32 devices in a mesh: inner: 8 (over z, y), target: 4 (over x, core).
Axes of the slice: x: 2, y: 2, z: 4, core: 2. Of those that a mesh axis runs over, the one named last changes fastest.
Arguments:
- left_factors: float32 [32, 32, 1024, 64], P('target', 'inner'), may hold values from -6 to 6
- mid_factors: float32 [32, 32, 1024, 64], P('target', 'inner'), may hold values from -0.1875 to 0.1875
- row_factors: float32 [32, 1024, 64], P('inner'), may hold values from -6 to 6
- col_factors: float32 [32, 1024, 64], P('inner'), may hold values from -0.09375 to 0.09375
- lists: int32 [32, 32], P('target'), may hold values from -1 to 31, as said below
- sketch_right: float32 [1024, 128], replicated, may hold values from -0.046875 to 0.046875
- sketch_left: float32 [1024, 128], replicated, may hold values from -0.046875 to 0.046875
- diag_tile: float32 [1024, 1024], P(None, 'target'), as said below
Outputs:
- left_sketch: float32 [32, 1024, 128], P('target', 'inner')
- right_factor: float32 [32, 128, 1024], P('target', 'inner')
- core: float32 [32, 128, 128], P('target', 'inner')
The draws below stay inside these ranges and needn't reach their ends.
Inputs may be any that keep to these rules, and one draw needn't show every extreme that they name: `lists`: row t holds each contributing inner index once in any order and -1 in the other slots; the contributing indices of a row are 0 to c - 1 for some count c of 1 to 32, and some row has all 32. `diag_tile`: upper triangular with diagonal entries of 1 to 2.
All inputs are finite; a program needn't handle non-finite values.
Results may differ from the reference program's by a relative error of at most 0.0003.
Values sent between devices are 32-bit elements; how exact they have to be, the bound alone decides.
No kernel may reach another device: no remote copies, remote signals or barrier semaphores. Data moves between devices by JAX's collectives and lax.ppermute only.
A program may use at most 128 MiB of HBM per device.

```python
import jax
import jax.numpy as jnp
from jax import lax

B = 1024
R = 64
S = 128
TGT = 32
INNER = 32


def draw_lists(key, part):
    count_key, pick_key, perm_key = jax.random.split(jax.random.fold_in(key, 17), 3)
    counts = jax.random.randint(count_key, (TGT,), 1, INNER + 1)
    chosen = jax.random.randint(pick_key, (), 0, TGT)
    counts = jnp.where(jnp.arange(TGT) == chosen, INNER, counts)
    perm_keys = jax.random.split(perm_key, TGT)
    orders = jax.vmap(lambda k: jax.random.permutation(k, INNER))(perm_keys).astype(jnp.int32)
    return jnp.where(orders < counts[:, None], orders, -1).astype(jnp.int32)


def draw_diag_tile(key, part):
    off_key, dia_key = jax.random.split(jax.random.fold_in(key, 29))
    upper = jax.random.normal(off_key, (B, B), jnp.float32) * 0.6 * (1.0 / B) ** 0.5
    diagonal = jax.random.uniform(dia_key, (B,), jnp.float32, 1.0, 2.0)
    return (jnp.triu(upper, 1) + jnp.diag(diagonal)).astype(jnp.float32)


def block_scale(rng, dims, cuts, smallest, largest):
    level, own = 1.0, jax.random.fold_in(rng, 6)
    for dim, blocks in cuts:
        draws = jnp.exp(jax.random.uniform(jax.random.fold_in(own, dim), (blocks,), jnp.float32, smallest / len(cuts), largest / len(cuts)))
        level = level * jnp.repeat(draws, dims[dim] // blocks).reshape([-1 if axis == dim else 1 for axis in range(len(dims))])
    return level


def noise(stream_key, shape, deviation, reach, cuts=(), kind=jnp.bfloat16):
    loudness = block_scale(stream_key, shape, cuts, -0.22, 0.18) if cuts else 1.0
    values = jax.random.normal(stream_key, shape, jnp.float32) * deviation * loudness
    return jnp.minimum(jnp.maximum(values, -reach), reach).astype(kind)


def setup_inputs(seed: int = 0) -> dict:
    key_of = jax.random.split(jax.random.key(seed), 9)
    return {
        "left_factors": noise(key_of[0], (TGT, INNER, B, R), 1.0, 6.0, ((0, 4), (1, 8)), jnp.float32),
        "mid_factors": noise(key_of[1], (TGT, INNER, B, R), B ** -0.5, 0.1875, ((0, 4), (1, 8)), jnp.float32),
        "row_factors": noise(key_of[2], (INNER, B, R), 1.0, 6.0, ((0, 8),), jnp.float32),
        "col_factors": noise(key_of[3], (INNER, B, R), (64 * R) ** -0.5, 0.09375, ((0, 8),), jnp.float32),
        "lists": draw_lists(jax.random.fold_in(key_of[8], 71), 0),
        "sketch_right": noise(key_of[5], (B, S), (16 * B) ** -0.5, 0.046875, (), jnp.float32),
        "sketch_left": noise(key_of[6], (B, S), (16 * B) ** -0.5, 0.046875, (), jnp.float32),
        "diag_tile": draw_diag_tile(jax.random.fold_in(key_of[8], 71), 0),
    }


precision_top = lax.Precision.HIGHEST

def reference(left_factors, mid_factors, row_factors, col_factors, lists, sketch_right, sketch_left, diag_tile):
    inner_ids = jnp.arange(INNER, dtype=jnp.int32)
    col_sketch = jnp.einsum('kbr,bs->krs', col_factors, sketch_right, precision=precision_top)

    def one_target(items):
        left_tile, mid_tile, row_list = items
        present = jnp.sum((row_list[:, None] == inner_ids[None, :]).astype(jnp.float32), axis=0)
        coupling = jnp.einsum('kbr,kbq->krq', mid_tile, row_factors, precision=precision_top) * present[:, None, None]
        inner_left = jnp.einsum('krq,kqs->krs', coupling, col_sketch, precision=precision_top)
        left_out = jnp.einsum('kbr,krs->bs', left_tile, inner_left, precision=precision_top)
        projected = jnp.einsum('bs,kbr->ksr', sketch_left, left_tile, precision=precision_top)
        joined = jnp.einsum('ksr,krq->ksq', projected, coupling, precision=precision_top)
        right_sketch = jnp.einsum('ksq,kbq->sb', joined, col_factors, precision=precision_top)
        core_out = jnp.dot(right_sketch, sketch_right, precision=precision_top)
        solved = lax.linalg.triangular_solve(diag_tile, right_sketch, left_side=False, lower=False)
        return (left_out, solved, core_out)
    return lax.map(one_target, (left_factors, mid_factors, lists))
```

```python
import functools

import jax
import jax.numpy as jnp
from jax import lax
from jax.experimental import pallas as pl
from jax.experimental.pallas import tpu as pltpu
from jax.sharding import PartitionSpec as P


f32 = jnp.float32
bf16 = jnp.bfloat16
precision_top = lax.Precision.HIGHEST
NN = (((1,), (0,)), ((), ()))
NT = (((1,), (1,)), ((), ()))


def split(x):
    high = x.astype(bf16)
    return high, (x - high.astype(f32)).astype(bf16)


def dot3(a, b, dims=NN):
    dot = functools.partial(lax.dot_general, dimension_numbers=dims, preferred_element_type=f32)
    return dot(a[0], b[0]) + (dot(a[0], b[1]) + dot(a[1], b[0]))


def dest_order(n, first):
    bits = n.bit_length() - 1
    order = [first] + [b for b in range(bits) if b != first]
    out = []
    for j in range(n):
        d = 0
        for pos, b in enumerate(order):
            d |= ((j >> (bits - 1 - pos)) & 1) << b
        out.append(d)
    return out


def partial_kernel(n, zl, me_ref, lists_ref, mid_ref, left_ref, row_ref, col_ref, sl_ref, sr_ref,
                   lkeep_ref, lsend_ref, jkeep_ref, jsend_ref,
                   row_s, sl_s, csk_s, l_s, j_s):
    local, rank, order = mid_ref.shape[1:]
    wide = local * rank
    me = me_ref[0]

    @pl.when(pl.program_id(0) == 0)
    def _():
        row_s[0], row_s[1] = split(row_ref[...].reshape(wide, order))
        sl = split(sl_ref[...])
        sl_s[0], sl_s[1] = sl
        csk = dot3(split(col_ref[...].reshape(wide, order)), split(sr_ref[...]))
        csk_s[0], csk_s[1] = split(csk)

    t = me_ref[1] + pl.program_id(0)
    lists = lists_ref[pl.ds(t, 1), :]
    lane_k = lax.broadcasted_iota(jnp.int32, (1, wide), 1) // rank
    present = jnp.zeros((1, wide), f32)
    for k in range(local):
        hit = jnp.sum(jnp.where(lists == me * local + k, 1.0, 0.0), axis=1, keepdims=True)
        present = jnp.where(lane_k == k, hit, present)
    row_k = lax.broadcasted_iota(jnp.int32, (wide, wide), 0) // rank
    col_k = lax.broadcasted_iota(jnp.int32, (wide, wide), 1) // rank

    mid = split(mid_ref[0].reshape(wide, order))
    coupling = dot3(mid, (row_s[0], row_s[1]), NT)
    coupling = split(jnp.where(row_k == col_k, coupling * present, 0.0))
    inner = dot3(coupling, (csk_s[0], csk_s[1]))
    left = split(left_ref[0].reshape(wide, order))
    left_t = dot3(split(inner.T), left)
    l_s[...] = left_t.T
    projected = dot3(left, (sl_s[0], sl_s[1]))
    j_s[...] = dot3(split(projected.T), coupling)
    width = order // n
    rows = j_s.shape[0] // n
    half = n // 2
    for j, d in enumerate(dest_order(n, 0)):
        piece = l_s[pl.ds(pl.multiple_of((me ^ d) * width, width), width), :]
        if j < half:
            lkeep_ref[j, 0] = piece
        else:
            lsend_ref[j - half, 0] = piece
    for j, d in enumerate(dest_order(n, zl)):
        piece = j_s[pl.ds(pl.multiple_of((me ^ d) * rows, rows), rows), :]
        if j < half:
            jkeep_ref[j, 0] = piece
        else:
            jsend_ref[j - half, 0] = piece


def partials(n, zl, me, t0, count, lists, mid, left, row, col, sl, sr):
    _, local, rank, order = mid.shape
    cols = sl.shape[1]
    wide = local * rank
    half = n // 2
    info = jnp.stack([me, jnp.int32(t0)])

    def whole(a):
        return pl.BlockSpec(a.shape, lambda i, s: (0,) * a.ndim)

    big = pl.BlockSpec((1, local, rank, order), lambda i, s: (t0 + i, 0, 0, 0))
    lspec = pl.BlockSpec((half, 1, order // n, cols), lambda i, s: (0, i, 0, 0))
    jspec = pl.BlockSpec((half, 1, cols // n, wide), lambda i, s: (0, i, 0, 0))
    lshape = jax.ShapeDtypeStruct((half, count, order // n, cols), f32)
    jshape = jax.ShapeDtypeStruct((half, count, cols // n, wide), f32)
    return pl.pallas_call(
        functools.partial(partial_kernel, n, zl),
        grid_spec=pltpu.PrefetchScalarGridSpec(
            num_scalar_prefetch=1,
            grid=(count,),
            in_specs=[whole(lists), big, big, whole(row), whole(col), whole(sl), whole(sr)],
            out_specs=[lspec, lspec, jspec, jspec],
            scratch_shapes=[
                pltpu.VMEM((2, wide, order), bf16),
                pltpu.VMEM((2, order, cols), bf16),
                pltpu.VMEM((2, wide, cols), bf16),
                pltpu.VMEM((order, cols), f32),
                pltpu.VMEM((cols, wide), f32),
            ],
        ),
        out_shape=[lshape, lshape, jshape, jshape],
        cost_estimate=pl.CostEstimate(
            flops=count * 2 * 3 * wide * order * (wide + 2 * cols), transcendentals=0,
            bytes_accessed=4 * (count * (2 * wide * order + order * cols) + 4 * wide * order),
        ),
        name="partials",
    )(info, lists, mid, left, row, col, sl, sr)


def product_kernel(pieces, core_ref, *refs):
    jk = refs[:pieces]
    jr = refs[pieces:2 * pieces]
    own_ref, got_ref, other_ref, keep_ref, send_ref = refs[2 * pieces:]
    core = core_ref[0]
    own = split(own_ref[...])
    got = split(got_ref[...])
    other = split(other_ref[...])
    share = got_ref.shape[0]
    quarter = keep_ref.shape[0]
    t = 0
    for p in range(pieces):
        half, count, rows, wide = jk[p].shape
        m = half * count * rows
        out = dot3(split(jk[p][...].reshape(m, wide)), own)
        flat = jr[p]
        a = flat[:, :, :, pl.ds(pl.multiple_of(core * share, share), share)].reshape(m, share)
        b = flat[:, :, :, pl.ds(pl.multiple_of((1 - core) * share, share), share)].reshape(m, share)
        out = out + dot3(split(a), got) + dot3(split(b), other)
        out = out.reshape(half, count, rows, out.shape[1])
        keep_ref[:, t:t + count] = out[:quarter]
        send_ref[:, t:t + count] = out[quarter:]
        t += count


def product(core, jkeep, jrecv, own, got, other):
    pieces = len(jkeep)
    half, _, rows, wide = jkeep[0].shape
    total = sum(j.shape[1] for j in jkeep)
    order = own.shape[1]
    tile = min(256, order)

    def whole(a):
        return pl.BlockSpec(a.shape, lambda i, s: (0,) * a.ndim)

    def wtile(a):
        return pl.BlockSpec((a.shape[0], tile), lambda i, s: (0, i))

    ospec = pl.BlockSpec((half // 2, total, rows, tile), lambda i, s: (0, 0, 0, i))
    oshape = jax.ShapeDtypeStruct((half // 2, total, rows, order), f32)
    return pl.pallas_call(
        functools.partial(product_kernel, pieces),
        grid_spec=pltpu.PrefetchScalarGridSpec(
            num_scalar_prefetch=1,
            grid=(order // tile,),
            in_specs=[whole(j) for j in jkeep + jrecv] + [wtile(own), wtile(got), wtile(other)],
            out_specs=[ospec, ospec],
        ),
        out_shape=[oshape, oshape],
        cost_estimate=pl.CostEstimate(
            flops=2 * 3 * half * total * rows * 2 * wide * order, transcendentals=0,
            bytes_accessed=4 * (2 * wide * order + half * total * rows * (2 * wide + order)),
        ),
        name="product",
    )(core.reshape(1), *jkeep, *jrecv, own, got, other)


def inverse_kernel(parts, base, me_ref, *refs):
    blocks = refs[:parts]
    inv_ref, d_s = refs[parts:]
    order = d_s.shape[0]
    width = blocks[0].shape[1]
    dot = functools.partial(jnp.dot, precision=precision_top, preferred_element_type=f32)
    for d in range(parts):
        d_s[:, pl.ds(pl.multiple_of((me_ref[0] ^ d) * width, width), width)] = blocks[d][...]
    inv_ref[...] = jnp.zeros_like(inv_ref)
    r = lax.broadcasted_iota(jnp.int32, (base, base), 0)
    c = lax.broadcasted_iota(jnp.int32, (base, base), 1)
    xs = []
    tiles = []
    for b in range(order // base):
        tile = d_s[b * base:(b + 1) * base, b * base:(b + 1) * base]
        tiles.append(tile)
        xs.append(jnp.where(r == c, 1.0 / jnp.where(r == c, tile, 1.0), 0.0))
    w = 1
    while w < base:
        upper = (r // (2 * w) == c // (2 * w)) & (r // w < c // w)
        for b in range(order // base):
            step = dot(dot(xs[b], jnp.where(upper, tiles[b], 0.0)), xs[b])
            xs[b] = xs[b] - step
        w *= 2
    for b in range(order // base):
        inv_ref[b * base:(b + 1) * base, b * base:(b + 1) * base] = xs[b]
    while w < order:
        for s in range(0, order, 2 * w):
            a, m, e = s, s + w, s + 2 * w
            step = dot(inv_ref[a:m, a:m], d_s[a:m, m:e])
            inv_ref[a:m, m:e] = -dot(step, inv_ref[m:e, m:e])
        w *= 2


def inverse(me, blocks):
    order = blocks[0].shape[0]
    return pl.pallas_call(
        functools.partial(inverse_kernel, len(blocks), min(128, order)),
        grid_spec=pltpu.PrefetchScalarGridSpec(
            num_scalar_prefetch=1,
            grid=(1,),
            in_specs=[pl.BlockSpec(b.shape, lambda i, s: (0, 0)) for b in blocks],
            out_specs=pl.BlockSpec((order, order), lambda i, s: (0, 0)),
            scratch_shapes=[pltpu.VMEM((order, order), f32)],
        ),
        out_shape=jax.ShapeDtypeStruct((order, order), f32),
        cost_estimate=pl.CostEstimate(flops=12 * order * order * 512, transcendentals=0,
                                      bytes_accessed=8 * order * order),
        name="inverse",
    )(me.reshape(1), *blocks)


def finish_kernel(a_ref, b_ref, c_ref, inv_ref, sr_ref, out_ref, core_ref):
    total, rows, order = a_ref.shape
    right = (a_ref[...] + b_ref[...] + c_ref[...]).reshape(total * rows, order)
    dot = functools.partial(jnp.dot, precision=precision_top, preferred_element_type=f32)
    out_ref[...] = dot(right, inv_ref[...]).reshape(out_ref.shape)

    @pl.when(pl.program_id(0) == 0)
    def _():
        core_ref[...] = dot(right, sr_ref[...]).reshape(core_ref.shape)


def finish(a, b, c, inv, sr):
    total, rows, order = a.shape
    tile = min(256, order)

    def whole(x):
        return pl.BlockSpec(x.shape, lambda i: (0,) * x.ndim)

    return pl.pallas_call(
        finish_kernel,
        grid=(order // tile,),
        in_specs=[whole(a), whole(b), whole(c), pl.BlockSpec((order, tile), lambda i: (0, i)), whole(sr)],
        out_specs=[
            pl.BlockSpec((total, rows, tile), lambda i: (0, 0, i)),
            pl.BlockSpec((total, rows, sr.shape[1]), lambda i: (0, 0, 0)),
        ],
        out_shape=[
            jax.ShapeDtypeStruct((total, rows, order), f32),
            jax.ShapeDtypeStruct((total, rows, sr.shape[1]), f32),
        ],
        cost_estimate=pl.CostEstimate(flops=12 * total * rows * order * order, transcendentals=0,
                                      bytes_accessed=4 * order * order),
        name="finish",
    )(a, b, c, inv, sr)


def swap(x, axis, size, bit):
    return lax.ppermute(x, axis, [(i, i ^ bit) for i in range(size)])


def on_device(n, n_target, left_factors, mid_factors, row_factors, col_factors, lists,
              sketch_right, sketch_left, diag_tile):
    me = lax.axis_index("inner").astype(jnp.int32)
    my_target = lax.axis_index("target").astype(jnp.int32)
    core = my_target & 1
    bits = n.bit_length() - 1
    zl = max(bits - 2, 0)
    flip = functools.partial(jnp.swapaxes, axis1=2, axis2=3)
    left, mid = flip(left_factors), flip(mid_factors)
    row, col = jnp.swapaxes(row_factors, 1, 2), jnp.swapaxes(col_factors, 1, 2)
    targets, local, rank, order = left.shape
    wide = local * rank
    own = col.reshape(wide, order)
    share = wide // 2

    mine = lax.dynamic_slice_in_dim(own, core * share, share, 0)
    got = swap(mine, "inner", n, 1 << zl)
    other = swap(got, "target", n_target, 1)
    blocks = [diag_tile]
    by_delta = {0: diag_tile}
    bit = n_target // 2
    while bit:
        for d, block in list(by_delta.items()):
            by_delta[d ^ bit] = swap(block, "target", n_target, bit)
        bit //= 2
    blocks = [by_delta[d] for d in range(n_target)]

    size = max(targets // 4, 1)
    group = 2
    starts = list(range(0, targets, size))
    parts = [partials(n, zl, me, t0, size, lists, mid, left, row, col, sketch_left, sketch_right)
             for t0 in starts]
    jrecv = [swap(p[3], "inner", n, 1 << zl) for p in parts]
    inv = inverse(my_target, blocks)

    rest = [b for b in range(bits) if b != zl]
    solved, cores = [], []
    for g in range(0, len(parts), group):
        keep, send = product(core, [p[2] for p in parts[g:g + group]], jrecv[g:g + group], own, got, other)
        terms = [keep]
        for pos, b in enumerate(rest):
            terms.append(swap(send, "inner", n, 1 << b))
            if pos + 1 < len(rest):
                cut = terms[0].shape[0] // 2
                send = sum(x[cut:] for x in terms)
                terms = [x[:cut] for x in terms]
        terms = [x[0] for x in terms]
        while len(terms) > 3:
            terms = [terms[0] + terms[1]] + terms[2:]
        out, small = finish(*terms, inv, sketch_right)
        solved.append(out)
        cores.append(small)

    lefts = []
    for keep, send, _, _ in parts:
        terms = [keep]
        for b in range(bits):
            terms.append(swap(send, "inner", n, 1 << b))
            if b + 1 < bits:
                cut = terms[0].shape[0] // 2
                send = sum(x[cut:] for x in terms)
                terms = [x[:cut] for x in terms]
        lefts.append(sum(x[0] for x in terms))
    return (jnp.concatenate(lefts, 0), jnp.concatenate(solved, 0), jnp.concatenate(cores, 0))


def solution(mesh):
    placed = (
        P("target", "inner", None, None),
        P("target", "inner", None, None),
        P("inner", None, None),
        P("inner", None, None),
        P("target", None),
        P(),
        P(),
        P(None, "target"),
    )
    return jax.shard_map(
        functools.partial(on_device, mesh.shape["inner"], mesh.shape["target"]),
        mesh=mesh,
        in_specs=placed,
        out_specs=(
            P("target", "inner", None),
            P("target", "inner", None),
            P("target", "inner", None),
        ),
        check_vma=False,
    )
```
